32 devices in a mesh: groups: 2 (over y), seq: 4 (over z), head: 2 (over x), rep: 2 (over core).
Axes of the slice: x: 2, y: 2, z: 4, core: 2. Of those that a mesh axis runs over, the one named last changes fastest.
Arguments:
- query_proj: bfloat16 [2048, 4096], P(('groups', 'seq'), ('head', 'rep')), parts along dimension 0, may hold values from -6 to 6
- key_proj: bfloat16 [2048, 4096], P(('groups', 'seq'), ('head', 'rep')), parts along dimension 0, may hold values from -6 to 6
- value_proj: bfloat16 [2048, 4096], P(('groups', 'seq'), ('head', 'rep')), parts along dimension 0, may hold values from -6 to 6
- forget_logits: bfloat16 [2048, 4096], P(('groups', 'seq'), ('head', 'rep')), parts along dimension 0, may hold values from -8 to 8
- decay_rate: float32 [4096], P(('head', 'rep')), may hold values from 0.001 to 0.1
- beta_logits: bfloat16 [2048, 32], P(('groups', 'seq'), ('head', 'rep')), parts along dimension 0, may hold values from -4.5 to -0.5
- gate_logits: bfloat16 [2048, 4096], P(('groups', 'seq'), ('head', 'rep')), parts along dimension 0, may hold values from -6 to 6
- norm_gain: float32 [128], replicated, may hold values from 0.25 to 1.75
- out_weight: bfloat16 [4096, 2304], P(('head', 'rep')), may hold values from -0.125 to 0.125
- stream_starts: int32 [16], P('groups'), parts along dimension 0, may hold values from 0 to 1023, as said below
- stream_slots: int32 [16], P('groups'), parts along dimension 0, may hold values from 0 to 7, each once
Outputs:
- layer_out: bfloat16 [2048, 2304], P(('groups', 'seq'), ('head', 'rep')), parts along dimension 0
- slot_states: bfloat16 [16, 32, 128, 128], P(('groups', 'seq'), ('head', 'rep')), parts along dimension 0
The draws below stay inside these ranges and needn't reach their ends.
There are 2 independent parts, one for each index of `groups`. The reference program is written for one: setup_inputs(seed, part) draws one part's arguments, and reference() takes and returns one part's arrays. A program takes and returns all parts, laid end to end along the dimension named above; an argument that names none is the same for every part. Nothing has to cross between parts.
Inputs may be any that keep to these rules, and one draw needn't show every extreme that they name: `stream_starts`: strictly increasing, the first is 0; at most 4 streams end within one index of seq's 256 tokens, and in every draw some index has exactly 4 ends. `stream_slots`: each slot once; slot s is kept by index s // 2 of seq.
All inputs are finite; a program needn't handle non-finite values.
Results may differ from the reference program's by a relative error of at most 0.014.
Values may be sent and summed in bfloat16 or wider, within the bound.
A program may use at most 64 MiB of HBM per device.

```python
import math
import jax
import jax.numpy as jnp
from jax import lax

HEAD_TOTAL = 32
KEY_SIZE = 128
DV = 128
D = 2304
TOKEN_PER_PART = 256
STREAMS_DEV = 2
HEAD_GROUPS = 4
HEADS_DEV = 8
TOKEN_TOTAL = 1024
STREAMS = 8


def shared_pair(key):
    first_key, second_key = jax.random.split(jax.random.fold_in(key, 11))
    common_key = jax.random.fold_in(key, 13)
    full_shape = (TOKEN_TOTAL, HEAD_TOTAL * KEY_SIZE)
    opening_sample = jax.random.normal(first_key, full_shape, jnp.float32)
    second_draw = jax.random.normal(second_key, full_shape, jnp.float32)
    common = jax.random.normal(common_key, (HEAD_TOTAL, KEY_SIZE), jnp.float32)
    common_rows = jnp.broadcast_to(common.reshape(1, HEAD_TOTAL * KEY_SIZE), full_shape)
    key_rows = 0.8 * common_rows + 0.6 * opening_sample
    query_rows = 0.6 * key_rows + 0.8 * second_draw
    return (jnp.clip(key_rows, -6.0, 6.0), jnp.clip(query_rows, -6.0, 6.0))


def draw_key_proj(key, part):
    return shared_pair(key)[0].astype(jnp.bfloat16)


def draw_query_proj(key, part):
    return shared_pair(key)[1].astype(jnp.bfloat16)


def draw_forget_logits(key, part):
    root_random_key, offset_random_key, spell_random_key, location_random_key = jax.random.split(jax.random.fold_in(key, 21), 4)
    shards = TOKEN_TOTAL // TOKEN_PER_PART
    opening_sample = -1.0 + 0.7 * jax.random.normal(root_random_key, (TOKEN_TOTAL, HEAD_TOTAL * KEY_SIZE), jnp.float32)
    shifts = jax.random.uniform(offset_random_key, (shards, 1, HEAD_TOTAL * KEY_SIZE), jnp.float32, -0.6, 0.6)
    opening_sample = (opening_sample.reshape(shards, TOKEN_PER_PART, HEAD_TOTAL * KEY_SIZE) + shifts).reshape(TOKEN_TOTAL, HEAD_TOTAL * KEY_SIZE)
    spell_runs = max(2, TOKEN_TOTAL // 2048)
    spell_length = max(2, min(32, TOKEN_PER_PART // 4))
    stream_begins = jax.random.randint(location_random_key, (spell_runs,), 0, TOKEN_TOTAL - spell_length + 1)
    token_positions = jnp.arange(TOKEN_TOTAL)
    within_flags = jnp.any((token_positions[:, None] >= stream_begins[None, :]) & (token_positions[:, None] < stream_begins[None, :] + spell_length), axis=1)
    spell_value_rows = 7.0 + 0.5 * jax.random.uniform(spell_random_key, (TOKEN_TOTAL, HEAD_TOTAL * KEY_SIZE), jnp.float32, -1.0, 1.0)
    return jnp.clip(jnp.where(within_flags[:, None], spell_value_rows, opening_sample), -8.0, 8.0).astype(jnp.bfloat16)


def draw_decay_rate(key, part):
    slow_key = jax.random.fold_in(jax.random.fold_in(key, 41), 1)
    log_rates = jax.random.uniform(slow_key, (HEAD_TOTAL * KEY_SIZE,), jnp.float32, math.log(0.001), math.log(0.1))
    return jnp.clip(jnp.exp(log_rates), 0.001, 0.1).astype(jnp.float32)


def draw_stream_starts(key, part):
    shards = TOKEN_TOTAL // TOKEN_PER_PART
    pair_count = shards // 2
    most_ends = 2 * STREAMS_DEV
    count_key, force_key, location_random_key = jax.random.split(jax.random.fold_in(key, 31), 3)
    firsts = jax.random.randint(count_key, (pair_count,), 0, most_ends + 1)
    pair_ids = jnp.arange(pair_count)
    firsts = jnp.where(pair_ids == pair_count - 1, jnp.minimum(firsts, most_ends - 1), firsts)
    forced = jax.random.randint(force_key, (), 0, pair_count)
    pinned = jnp.where(forced == pair_count - 1, 0, most_ends)
    firsts = jnp.where(pair_ids == forced, pinned, firsts)
    counts = jnp.stack([firsts, most_ends - firsts], axis=1).reshape(shards)
    orders = jax.vmap(lambda sub_key: jax.random.permutation(sub_key, TOKEN_PER_PART))(jax.random.split(location_random_key, shards))
    tail_row = orders[shards - 1]
    last_rank = tail_row[TOKEN_PER_PART - 1]
    token_positions = jnp.arange(TOKEN_PER_PART)
    tail_row = jnp.where(token_positions == TOKEN_PER_PART - 1, -1, jnp.where(tail_row > last_rank, tail_row - 1, tail_row))
    orders = orders.at[shards - 1].set(tail_row)
    limits = counts - (jnp.arange(shards) == shards - 1).astype(counts.dtype)
    ending = (orders < limits[:, None]).reshape(TOKEN_TOTAL)
    rank_of = jnp.cumsum(ending.astype(jnp.int32)) - 1
    targets = jnp.where(ending, rank_of, STREAMS)
    finals = jnp.zeros((STREAMS,), jnp.int32).at[targets].set(jnp.arange(TOKEN_TOTAL, dtype=jnp.int32), mode='drop')
    return jnp.concatenate([jnp.zeros((1,), jnp.int32), finals[:-1] + 1]).astype(jnp.int32)


def strengthened(array, stream_key, source, target, shards_of, factor):
    owner, partner = [(jnp.arange(array.shape[dim]) // (array.shape[dim] // shards_of)).reshape([-1 if axis == dim else 1 for axis in range(array.ndim)]) for dim in (source, target)]
    chosen = jax.random.permutation(stream_key, shards_of)[partner]
    strong = (owner == chosen) | (owner == (partner + shards_of // 2) % shards_of)
    return jnp.where(strong, factor * array, array)


def block_scale(own_key, extent, cuts, low, top_value):
    factor_of, own = 1.0, jax.random.fold_in(own_key, 6)
    for axis_at, parts in cuts:
        steps = jnp.exp(jax.random.uniform(jax.random.fold_in(own, axis_at), (parts,), jnp.float32, low / len(cuts), top_value / len(cuts)))
        factor_of = factor_of * jnp.repeat(steps, extent[axis_at] // parts).reshape([-1 if axis == axis_at else 1 for axis in range(len(extent))])
    return factor_of


def normal_values(stream_key, shape, spread, most, cuts=(), kind=jnp.bfloat16):
    factor_of = block_scale(stream_key, shape, cuts, -0.22, 0.18) if cuts else 1.0
    result = jax.random.normal(stream_key, shape, jnp.float32) * spread * factor_of
    return jnp.minimum(jnp.maximum(result, -most), most).astype(kind)


def gaussian_with(rng, extent, deviation, bound, cuts, heavy, kind=jnp.bfloat16):
    values = deviation * jax.random.normal(rng, extent, jnp.float32)
    if cuts:
        values = values * block_scale(rng, extent, cuts, -0.22, 0.18)
    return jnp.clip(strengthened(values, jax.random.fold_in(rng, 3), *heavy), -bound, bound).astype(kind)


def setup_inputs(seed: int = 0, part: int = 0) -> dict:
    streams_of = jax.random.split(jax.random.key(seed), 12)
    part_splits = jax.random.split(jax.random.fold_in(streams_of[11], part), 12)
    return {
        "query_proj": draw_query_proj(jax.random.fold_in(jax.random.fold_in(streams_of[11], part), 71), part),
        "key_proj": draw_key_proj(jax.random.fold_in(jax.random.fold_in(streams_of[11], part), 71), part),
        "value_proj": normal_values(part_splits[2], (TOKEN_TOTAL, HEAD_TOTAL * DV), 1.0, 6.0, ((0, 4), (1, 4))),
        "forget_logits": draw_forget_logits(jax.random.fold_in(jax.random.fold_in(streams_of[11], part), 71), part),
        "decay_rate": draw_decay_rate(jax.random.fold_in(streams_of[11], 71), part),
        "beta_logits": jnp.clip(-4.5 + 4.0 * jax.random.uniform(part_splits[5], (TOKEN_TOTAL, HEAD_TOTAL), jnp.float32) ** block_scale(part_splits[5], (TOKEN_TOTAL, HEAD_TOTAL), ((0, 4), (1, 4)), -0.2, 0.2), -4.5, -0.5).astype(jnp.bfloat16),
        "gate_logits": normal_values(part_splits[6], (TOKEN_TOTAL, HEAD_TOTAL * DV), 1.0, 6.0, ((0, 4), (1, 4))),
        "norm_gain": jnp.clip(1.0 + 0.15 * jax.random.normal(streams_of[7], (DV,), jnp.float32), 0.25, 1.75),
        "out_weight": gaussian_with(streams_of[8], (HEAD_TOTAL * DV, D), (HEAD_TOTAL * DV) ** -0.5, 0.125, ((0, 4),), (0, 1, 4, 2.0)),
        "stream_starts": draw_stream_starts(jax.random.fold_in(jax.random.fold_in(streams_of[11], part), 71), part),
        "stream_slots": jax.random.permutation(part_splits[10], STREAMS).astype(jnp.int32),
    }


SMALLEST_STEP = lax.Precision.HIGHEST

def unit_rows(rows, row_width):
    shaped = rows.astype(jnp.float32).reshape(rows.shape[0], -1, row_width)
    return shaped * lax.rsqrt(lax.optimization_barrier(jnp.sum(shaped * shaped, axis=-1, keepdims=True)) + 1e-06)

def reference(query_proj, key_proj, value_proj, forget_logits, decay_rate, beta_logits, gate_logits, norm_gain, out_weight, stream_starts, stream_slots):
    token_count = query_proj.shape[0]
    queries = unit_rows(query_proj, KEY_SIZE)
    keys_unit = unit_rows(key_proj, KEY_SIZE)
    values_all = value_proj.astype(jnp.float32).reshape(token_count, HEAD_TOTAL, DV)
    decays = jnp.exp(-decay_rate.reshape(HEAD_TOTAL, KEY_SIZE) * jax.nn.softplus(forget_logits.astype(jnp.float32).reshape(token_count, HEAD_TOTAL, KEY_SIZE)))
    betas = jax.nn.sigmoid(beta_logits.astype(jnp.float32))
    token_index = jnp.arange(token_count, dtype=jnp.int32)
    starting = jnp.any(token_index[:, None] == stream_starts[None, :], axis=1)
    ending = jnp.concatenate([starting[1:], jnp.ones((1,), dtype=bool)])
    stream_of = lax.optimization_barrier(jnp.sum((stream_starts[None, :] <= token_index[:, None]).astype(jnp.int32), axis=1)) - 1
    stream_ids = jnp.arange(STREAMS, dtype=jnp.int32)
    slot_of = lax.optimization_barrier(jnp.sum(jnp.where(stream_of[:, None] == stream_ids[None, :], stream_slots[None, :], 0), axis=1)).astype(jnp.int32)

    def advance(carry, slices):
        memory_state_matrix, slot_store = carry
        single_query_row, single_key_row, value_row, decay_row, beta_row, start_flag, end_flag, slot_index = slices
        memory_state_matrix = jnp.where(start_flag, jnp.zeros_like(memory_state_matrix), memory_state_matrix)
        memory_state_matrix = decay_row[:, :, None] * memory_state_matrix
        recalled_values = jnp.einsum('is,isq->iq', single_key_row, memory_state_matrix, precision=SMALLEST_STEP)
        memory_state_matrix = memory_state_matrix + beta_row[:, None, None] * single_key_row[:, :, None] * (value_row - recalled_values)[:, None, :]
        readout_row = jnp.einsum('is,isq->iq', single_query_row, memory_state_matrix, precision=SMALLEST_STEP)
        previous = lax.dynamic_index_in_dim(slot_store, slot_index, 0, keepdims=False)
        slot_store = lax.dynamic_update_index_in_dim(slot_store, jnp.where(end_flag, memory_state_matrix, previous), slot_index, 0)
        return ((memory_state_matrix, slot_store), readout_row)
    initial = (jnp.zeros((HEAD_TOTAL, KEY_SIZE, DV), jnp.float32), jnp.zeros((STREAMS, HEAD_TOTAL, KEY_SIZE, DV), jnp.float32))
    final_carry, read_out = lax.scan(advance, initial, (queries, keys_unit, values_all, decays, betas, starting, ending, slot_of))
    inverse_rms = lax.rsqrt(lax.optimization_barrier(jnp.mean(read_out * read_out, axis=-1, keepdims=True)) + 1e-05)
    gates = jax.nn.sigmoid(gate_logits.astype(jnp.float32).reshape(token_count, HEAD_TOTAL, DV))
    hidden = (read_out * inverse_rms * norm_gain * gates).reshape(token_count, HEAD_TOTAL * DV).astype(jnp.bfloat16)
    group_width = HEADS_DEV * DV
    summed = jnp.zeros((token_count, D), jnp.float32)
    for group_index in range(HEAD_GROUPS):
        lower_col = group_index * group_width
        partial_value = jnp.dot(hidden[:, lower_col:lower_col + group_width], out_weight[lower_col:lower_col + group_width], preferred_element_type=jnp.float32)
        rounded = lax.optimization_barrier(partial_value.astype(jnp.bfloat16))
        summed = summed + rounded.astype(jnp.float32)
    return (summed.astype(jnp.bfloat16), final_carry[1].astype(jnp.bfloat16))
```

```python
import functools
import jax
import jax.numpy as jnp
from jax import lax
from jax.experimental import pallas as pl
from jax.experimental.pallas import tpu as pltpu
from jax.sharding import PartitionSpec as P

ENDS_MAX = 4
STEP_HEADS = 2
BASE = 16
F32 = jnp.float32
BF16 = jnp.bfloat16
NN = (((1,), (0,)), ((), ()))
NT = (((1,), (1,)), ((), ()))


def halves(x):
    high = x.astype(BF16)
    return high, (x - high.astype(F32)).astype(BF16)


def mm1(a, b, dims=NN):
    return lax.dot_general(a.astype(BF16), b.astype(BF16), dims, preferred_element_type=F32)


def mm3(a, b, dims=NN):
    ah, al = halves(a)
    bh, bl = halves(b)
    dot = functools.partial(lax.dot_general, dimension_numbers=dims, preferred_element_type=F32)
    return dot(ah, bh) + (dot(ah, bl) + dot(al, bh))


def unit(x):
    return x * lax.rsqrt(jnp.sum(x * x, axis=-1, keepdims=True) + 1e-06)


def block_inverses(mats):
    size = mats[0].shape[0]
    row = lax.broadcasted_iota(jnp.int32, (size, size), 0)
    col = lax.broadcasted_iota(jnp.int32, (size, size), 1)
    eye = (row == col).astype(F32)
    inside = (row // BASE) == (col // BASE)
    powers = [jnp.where(inside, m, 0.0) for m in mats]
    result = [eye - p for p in powers]
    width = 2
    while width < BASE:
        powers = [mm3(p, p) for p in powers]
        result = [r + mm3(r, p) for r, p in zip(result, powers)]
        width *= 2
    width = BASE
    while width < size:
        off = ((row // (2 * width)) == (col // (2 * width))) & ((row // width) > (col // width))
        mids = [mm3(jnp.where(off, m, 0.0), r) for m, r in zip(mats, result)]
        result = [r - mm3(r, t) for r, t in zip(result, mids)]
        width *= 2
    return result


def local_kernel(info_ref, q_ref, k_ref, v_ref, f_ref, rate_ref, beta_ref, seg_col_ref, seg_row_ref,
                 out_ref, corr_ref, map_ref, tail_ref, end0_ref, ends_ref):
    length = q_ref.shape[0]
    half = length // 2
    step = pl.program_id(0)
    width = q_ref.shape[1] // STEP_HEADS
    before = info_ref[0]
    base = info_ref[1]
    ends = info_ref[2]
    seg_col = seg_col_ref[...]
    seg_row = seg_row_ref[...]
    row = lax.broadcasted_iota(jnp.int32, (length, length), 0)
    col = lax.broadcasted_iota(jnp.int32, (length, length), 1)
    same = seg_col == seg_row
    lower = same & (row >= col)
    strict = same & (row > col)
    first = (seg_col == before).astype(F32)
    first_row = (seg_row == before).astype(F32)
    sums = jnp.concatenate([(row >= col).astype(BF16), (same & (col > row)).astype(BF16)], axis=0)
    hrow = lax.broadcasted_iota(jnp.int32, (width, width), 0)
    hcol = lax.broadcasted_iota(jnp.int32, (width, width), 1)
    eye = (hrow == hcol).astype(F32)
    beta_all = jax.nn.sigmoid(beta_ref[...].astype(F32))
    lane = lax.broadcasted_iota(jnp.int32, beta_all.shape, 1)
    any_first = jnp.max(first_row)
    select = [
        ((seg_row == base + e) & (e < ends)).astype(F32) for e in range(ENDS_MAX)
    ] + [(seg_row == base + ends).astype(F32)]
    mats = []
    kept = []
    for i in range(STEP_HEADS):
        cols = slice(i * width, (i + 1) * width)
        q = unit(q_ref[:, cols].astype(F32))
        k = unit(k_ref[:, cols].astype(F32))
        x = f_ref[:, cols].astype(F32)
        soft = jnp.maximum(x, 0.0) + jnp.log1p(jnp.exp(-jnp.abs(x)))
        decay = -(rate_ref[:, cols] * soft)
        dh, dl = halves(decay)
        both = jnp.concatenate([dh, dl], axis=1)
        summed = lax.dot_general(sums, both, NN, preferred_element_type=F32)
        summed = summed[:, :width] + summed[:, width:]
        cum = summed[:length]
        suffix = jnp.exp(summed[length:])
        decayed = jnp.exp(cum)
        beta = jnp.sum(jnp.where(lane == step * STEP_HEADS + i, beta_all, 0.0), axis=1, keepdims=True)
        mid = cum[half - 1:half]
        parts = []
        scale = []
        for b in range(2):
            piece = cum[b * half:(b + 1) * half]
            center = 0.5 * (piece[:1] + piece[-1:])
            up = jnp.exp(piece - center)
            down = jnp.exp(center - piece)
            kb = k[b * half:(b + 1) * half]
            qb = q[b * half:(b + 1) * half]
            parts.append((jnp.concatenate([kb * up, qb * up], axis=0), kb * down))
            scale.append(center)
        blocks = [mm3(parts[b][0], parts[b][1], NT) for b in range(2)]
        cross = mm3(parts[1][0] * jnp.exp(scale[1] - mid), parts[0][1] * jnp.exp(mid - scale[0]), NT)
        coupling = [
            jnp.where(strict[b * half:(b + 1) * half, b * half:(b + 1) * half], blocks[b][:half], 0.0)
            * beta[b * half:(b + 1) * half]
            for b in range(2)
        ]
        coupling_cross = jnp.where(same[half:, :half], cross[:half], 0.0) * beta[half:]
        reading0 = jnp.where(lower[:half, :half], blocks[0][half:], 0.0)
        reading1 = jnp.where(lower[half:, half:], blocks[1][half:], 0.0)
        reading_cross = jnp.where(same[half:, :half], cross[half:], 0.0)
        right = jnp.concatenate([v_ref[:, cols].astype(F32) * beta, k * decayed * (beta * first)], axis=1)
        keep_row = jnp.exp(jnp.sum(first * decay, axis=0, keepdims=True))
        mats += coupling
        kept.append((coupling_cross, reading0, reading1, reading_cross, right,
                     q * decayed * first, (k * suffix).T, eye * (keep_row * any_first)))
    inverses = block_inverses(mats)
    for i in range(STEP_HEADS):
        cols = slice(i * width, (i + 1) * width)
        coupling_cross, reading0, reading1, reading_cross, right, query, key_end, diag = kept[i]
        u0 = mm3(inverses[2 * i], right[:half])
        u1 = mm3(inverses[2 * i + 1], right[half:] - mm3(coupling_cross, u0))
        u = jnp.concatenate([u0, u1], axis=0)
        r0 = mm3(reading0, u0)
        r1 = mm3(jnp.concatenate([reading_cross, reading1], axis=1), u)
        read = jnp.concatenate([r0, r1], axis=0)
        out_ref[:, cols] = read[:, :width]
        corr_ref[i] = (query - read[:, width:]).astype(corr_ref.dtype)
        lhs = jnp.concatenate([key_end * m for m in select], axis=0)
        states = mm1(lhs, u[:, :width])
        map_ref[i] = diag - mm1(key_end * first_row, u[:, width:])
        tail_ref[i] = states[ENDS_MAX * width:]
        end0_ref[i] = states[:width]
        for e in range(1, ENDS_MAX):
            ends_ref[e - 1, i] = states[e * width:(e + 1) * width].astype(BF16)


def local_math(q, k, v, f, rate, beta, seg, before, base, ends):
    length, total = q.shape
    heads = beta.shape[1]
    width = total // heads
    steps = heads // STEP_HEADS
    wide = pl.BlockSpec((length, STEP_HEADS * width), lambda n, s: (0, n))
    whole = lambda shape: pl.BlockSpec(shape, lambda n, s: (0, 0))
    cube = pl.BlockSpec((STEP_HEADS, width, width), lambda n, s: (n, 0, 0))
    info = jnp.stack([before, base, ends]).astype(jnp.int32)
    return pl.pallas_call(
        local_kernel,
        out_shape=(
            jax.ShapeDtypeStruct((length, total), F32),
            jax.ShapeDtypeStruct((heads, length, width), BF16),
            jax.ShapeDtypeStruct((heads, width, width), F32),
            jax.ShapeDtypeStruct((heads, width, width), F32),
            jax.ShapeDtypeStruct((heads, width, width), F32),
            jax.ShapeDtypeStruct((ENDS_MAX - 1, heads, width, width), BF16),
        ),
        grid_spec=pltpu.PrefetchScalarGridSpec(
            num_scalar_prefetch=1,
            grid=(steps,),
            in_specs=[wide, wide, wide, wide, pl.BlockSpec((1, STEP_HEADS * width), lambda n, s: (0, n)),
                      whole((length, heads)), whole((length, 1)), whole((1, length))],
            out_specs=(
                wide,
                pl.BlockSpec((STEP_HEADS, length, width), lambda n, s: (n, 0, 0)),
                cube, cube, cube,
                pl.BlockSpec((ENDS_MAX - 1, STEP_HEADS, width, width), lambda n, s: (0, n, 0, 0)),
            ),
        ),
        compiler_params=pltpu.CompilerParams(vmem_limit_bytes=48 << 20),
        name="local_math",
    )(info, q, k, v, f, rate.reshape(1, -1), beta, seg.reshape(-1, 1), seg.reshape(1, -1))


def from_behind(block, axis, distance):
    devices = range(lax.axis_size(axis))
    route = [(i - distance, i) for i in devices if i - distance in devices]
    return lax.ppermute(block, axis, route)


def per_device(query_proj, key_proj, value_proj, forget_logits, decay_rate, beta_logits,
               gate_logits, norm_gain, out_weight, stream_starts, stream_slots):
    length = query_proj.shape[0]
    heads = beta_logits.shape[1]
    width = decay_rate.shape[0] // heads
    devices = lax.axis_size("seq")
    place = lax.axis_index("seq")
    anchor = place * length
    positions = anchor + jnp.arange(length, dtype=jnp.int32)
    count = lambda mask: jnp.sum(mask.astype(jnp.int32))
    segments = jnp.sum((stream_starts[None, :] <= positions[:, None]).astype(jnp.int32), axis=1)
    before = count(stream_starts <= anchor - 1)
    before = jnp.where(place == 0, -1, before)
    later = stream_starts[1:]
    earlier = count(later <= anchor)
    ends = count((later > anchor) & (later <= anchor + length)) + (place == devices - 1).astype(jnp.int32)
    local, corr, maps, tail, end0, ends_rest = local_math(
        query_proj, key_proj, value_proj, forget_logits, decay_rate, beta_logits,
        segments, before, earlier + 1, ends)
    open_flag = (ends == 0).astype(F32)
    arriving = jnp.zeros((heads, width, width), BF16)
    maps16 = maps.astype(BF16)
    for _ in range(devices - 1):
        moved = jnp.matmul(maps16, arriving, preferred_element_type=F32)
        arriving = from_behind((tail + open_flag * moved).astype(BF16), "seq", 1)
    moved = jnp.matmul(maps16, arriving, preferred_element_type=F32)
    end0 = end0 + (1.0 - open_flag) * moved
    outputs = jnp.matmul(corr, arriving, preferred_element_type=F32).transpose(1, 0, 2) + local.reshape(length, heads, width)
    inverse_rms = lax.rsqrt(jnp.mean(outputs * outputs, axis=-1, keepdims=True) + 1e-05)
    gates = jax.nn.sigmoid(gate_logits.astype(F32).reshape(length, heads, width))
    hidden = (outputs * inverse_rms * norm_gain * gates).reshape(length, heads * width).astype(BF16)
    partial_value = jnp.dot(hidden, out_weight, preferred_element_type=F32)
    layer_out = lax.psum_scatter(partial_value.astype(BF16), ("head", "rep"), scatter_dimension=1, tiled=True)
    packed = jnp.concatenate([end0.astype(BF16)[None], ends_rest], axis=0)
    owned = stream_slots.shape[0] // devices
    ranks = jnp.arange(stream_slots.shape[0], dtype=jnp.int32) - earlier
    picks = jnp.arange(ENDS_MAX, dtype=jnp.int32)
    hit = (ranks[None, :] == picks[:, None]) & (picks < ends)[:, None]
    end_slots = jnp.sum(jnp.where(hit, stream_slots[None, :] + 1, 0), axis=1) - 1
    states = lax.all_gather(packed, "seq", axis=0, tiled=True)
    slots = lax.all_gather(end_slots, "seq", axis=0, tiled=True)
    chosen = (slots[None, :] == place * owned + jnp.arange(owned, dtype=jnp.int32)[:, None]).astype(BF16)
    slot_states = jnp.dot(chosen, states.reshape(states.shape[0], -1), preferred_element_type=F32)
    return (layer_out, slot_states.reshape(owned, heads, width, width).astype(BF16))


def solution(mesh):
    rows = P(("groups", "seq"), ("head", "rep"))
    in_specs = (rows, rows, rows, rows, P(("head", "rep")), rows, rows, P(),
                P(("head", "rep"), None), P("groups"), P("groups"))
    out_specs = (rows, P(("groups", "seq"), ("head", "rep"), None, None))
    return jax.shard_map(per_device, mesh=mesh, in_specs=in_specs, out_specs=out_specs, check_vma=False)
```

```python
import functools
import jax
import jax.numpy as jnp
from jax import lax
from jax.experimental import pallas as pl
from jax.experimental.pallas import tpu as pltpu
from jax.sharding import PartitionSpec as P

ENDS_MAX = 4
STEP_HEADS = 2
BASE = 16
F32 = jnp.float32
BF16 = jnp.bfloat16
NN = (((1,), (0,)), ((), ()))
NT = (((1,), (1,)), ((), ()))


def halves(x):
    high = x.astype(BF16)
    return high, (x - high.astype(F32)).astype(BF16)


def mm1(a, b, dims=NN):
    return lax.dot_general(a.astype(BF16), b.astype(BF16), dims, preferred_element_type=F32)


def mm3(a, b, dims=NN):
    ah, al = halves(a)
    bh, bl = halves(b)
    dot = functools.partial(lax.dot_general, dimension_numbers=dims, preferred_element_type=F32)
    return dot(ah, bh) + (dot(ah, bl) + dot(al, bh))


def unit(x):
    return x * lax.rsqrt(jnp.sum(x * x, axis=-1, keepdims=True) + 1e-06)


def block_inverses(mats):
    size = mats[0].shape[0]
    row = lax.broadcasted_iota(jnp.int32, (size, size), 0)
    col = lax.broadcasted_iota(jnp.int32, (size, size), 1)
    eye = (row == col).astype(F32)
    inside = (row // BASE) == (col // BASE)
    powers = [jnp.where(inside, m, 0.0) for m in mats]
    result = [eye - p for p in powers]
    width = 2
    while width < BASE:
        powers = [mm3(p, p) for p in powers]
        result = [r + mm3(r, p) for r, p in zip(result, powers)]
        width *= 2
    width = BASE
    while width < size:
        off = ((row // (2 * width)) == (col // (2 * width))) & ((row // width) > (col // width))
        mids = [mm3(jnp.where(off, m, 0.0), r) for m, r in zip(mats, result)]
        result = [r - mm3(r, t) for r, t in zip(result, mids)]
        width *= 2
    return result


def local_kernel(info_ref, q_ref, k_ref, v_ref, f_ref, rate_ref, beta_ref, seg_col_ref, seg_row_ref,
                 out_ref, corr_ref, map_ref, tail_ref, end0_ref, ends_ref):
    length = q_ref.shape[0]
    half = length // 2
    step = pl.program_id(0)
    width = q_ref.shape[1] // STEP_HEADS
    before = info_ref[0]
    base = info_ref[1]
    ends = info_ref[2]
    seg_col = seg_col_ref[...]
    seg_row = seg_row_ref[...]
    row = lax.broadcasted_iota(jnp.int32, (length, length), 0)
    col = lax.broadcasted_iota(jnp.int32, (length, length), 1)
    same = seg_col == seg_row
    lower = same & (row >= col)
    strict = same & (row > col)
    first = (seg_col == before).astype(F32)
    first_row = (seg_row == before).astype(F32)
    sums = jnp.concatenate([(row >= col).astype(BF16), (same & (col > row)).astype(BF16)], axis=0)
    hrow = lax.broadcasted_iota(jnp.int32, (width, width), 0)
    hcol = lax.broadcasted_iota(jnp.int32, (width, width), 1)
    eye = (hrow == hcol).astype(F32)
    beta_all = jax.nn.sigmoid(beta_ref[...].astype(F32))
    lane = lax.broadcasted_iota(jnp.int32, beta_all.shape, 1)
    any_first = jnp.max(first_row)
    select = [
        ((seg_row == base + e) & (e < ends)).astype(F32) for e in range(ENDS_MAX)
    ] + [(seg_row == base + ends).astype(F32)]
    mats = []
    kept = []
    for i in range(STEP_HEADS):
        cols = slice(i * width, (i + 1) * width)
        q = unit(q_ref[:, cols].astype(F32))
        k = unit(k_ref[:, cols].astype(F32))
        x = f_ref[:, cols].astype(F32)
        soft = jnp.maximum(x, 0.0) + jnp.log1p(jnp.exp(-jnp.abs(x)))
        decay = -(rate_ref[:, cols] * soft)
        dh, dl = halves(decay)
        both = jnp.concatenate([dh, dl], axis=1)
        summed = lax.dot_general(sums, both, NN, preferred_element_type=F32)
        summed = summed[:, :width] + summed[:, width:]
        cum = summed[:length]
        suffix = jnp.exp(summed[length:])
        decayed = jnp.exp(cum)
        beta = jnp.sum(jnp.where(lane == step * STEP_HEADS + i, beta_all, 0.0), axis=1, keepdims=True)
        mid = cum[half - 1:half]
        parts = []
        scale = []
        for b in range(2):
            piece = cum[b * half:(b + 1) * half]
            center = 0.5 * (piece[:1] + piece[-1:])
            up = jnp.exp(piece - center)
            down = jnp.exp(center - piece)
            kb = k[b * half:(b + 1) * half]
            qb = q[b * half:(b + 1) * half]
            parts.append((jnp.concatenate([kb * up, qb * up], axis=0), kb * down))
            scale.append(center)
        blocks = [mm3(parts[b][0], parts[b][1], NT) for b in range(2)]
        cross = mm3(parts[1][0] * jnp.exp(scale[1] - mid), parts[0][1] * jnp.exp(mid - scale[0]), NT)
        coupling = [
            jnp.where(strict[b * half:(b + 1) * half, b * half:(b + 1) * half], blocks[b][:half], 0.0)
            * beta[b * half:(b + 1) * half]
            for b in range(2)
        ]
        coupling_cross = jnp.where(same[half:, :half], cross[:half], 0.0) * beta[half:]
        reading0 = jnp.where(lower[:half, :half], blocks[0][half:], 0.0)
        reading1 = jnp.where(lower[half:, half:], blocks[1][half:], 0.0)
        reading_cross = jnp.where(same[half:, :half], cross[half:], 0.0)
        right = jnp.concatenate([v_ref[:, cols].astype(F32) * beta, k * decayed * (beta * first)], axis=1)
        keep_row = jnp.exp(jnp.sum(first * decay, axis=0, keepdims=True))
        mats += coupling
        kept.append((coupling_cross, reading0, reading1, reading_cross, right,
                     q * decayed * first, (k * suffix).T, eye * (keep_row * any_first)))
    inverses = block_inverses(mats)
    for i in range(STEP_HEADS):
        cols = slice(i * width, (i + 1) * width)
        coupling_cross, reading0, reading1, reading_cross, right, query, key_end, diag = kept[i]
        u0 = mm3(inverses[2 * i], right[:half])
        u1 = mm3(inverses[2 * i + 1], right[half:] - mm3(coupling_cross, u0))
        u = jnp.concatenate([u0, u1], axis=0)
        r0 = mm3(reading0, u0)
        r1 = mm3(jnp.concatenate([reading_cross, reading1], axis=1), u)
        read = jnp.concatenate([r0, r1], axis=0)
        out_ref[i] = read[:, :width]
        corr_ref[i] = (query - read[:, width:]).astype(corr_ref.dtype)
        lhs = jnp.concatenate([key_end * m for m in select], axis=0)
        states = mm1(lhs, u[:, :width])
        map_ref[i] = (diag - mm1(key_end * first_row, u[:, width:])).astype(map_ref.dtype)
        tail_ref[i] = states[ENDS_MAX * width:]
        end0_ref[i] = states[:width]
        for e in range(1, ENDS_MAX):
            ends_ref[i, e - 1] = states[e * width:(e + 1) * width].astype(BF16)


def local_math(q, k, v, f, rate, beta, seg, before, base, ends):
    length, total = q.shape
    heads = beta.shape[1]
    width = total // heads
    steps = heads // STEP_HEADS
    wide = pl.BlockSpec((length, STEP_HEADS * width), lambda n, s: (0, n))
    whole = lambda shape: pl.BlockSpec(shape, lambda n, s: (0, 0))
    cube = pl.BlockSpec((STEP_HEADS, width, width), lambda n, s: (n, 0, 0))
    info = jnp.stack([before, base, ends]).astype(jnp.int32)
    return pl.pallas_call(
        local_kernel,
        out_shape=(
            jax.ShapeDtypeStruct((heads, length, width), F32),
            jax.ShapeDtypeStruct((heads, length, width), BF16),
            jax.ShapeDtypeStruct((heads, width, width), BF16),
            jax.ShapeDtypeStruct((heads, width, width), F32),
            jax.ShapeDtypeStruct((heads, width, width), F32),
            jax.ShapeDtypeStruct((heads, ENDS_MAX - 1, width, width), BF16),
        ),
        grid_spec=pltpu.PrefetchScalarGridSpec(
            num_scalar_prefetch=1,
            grid=(steps,),
            in_specs=[wide, wide, wide, wide, pl.BlockSpec((1, STEP_HEADS * width), lambda n, s: (0, n)),
                      whole((length, heads)), whole((length, 1)), whole((1, length))],
            out_specs=(
                pl.BlockSpec((STEP_HEADS, length, width), lambda n, s: (n, 0, 0)),
                pl.BlockSpec((STEP_HEADS, length, width), lambda n, s: (n, 0, 0)),
                cube, cube, cube,
                pl.BlockSpec((STEP_HEADS, ENDS_MAX - 1, width, width), lambda n, s: (n, 0, 0, 0)),
            ),
        ),
        compiler_params=pltpu.CompilerParams(vmem_limit_bytes=48 << 20),
        name="local_math",
    )(info, q, k, v, f, rate.reshape(1, -1), beta, seg.reshape(-1, 1), seg.reshape(1, -1))


def finish_kernel(n, nh, scal_ref, sel_ref, local_ref, corr_ref, map_ref, tail_ref, end0_ref, rest_ref,
                  gate_ref, gain_ref, weight_hbm, layer_ref, slot_ref,
                  weight, hidden, parts, sums, pair_in, cross_in, state_out, state_in, own,
                  raw_r, raw_l, buf_r, buf_l,
                  weight_sem, st_send, st_recv, rr_send, rr_recv, rl_send, rl_recv,
                  r_send, r_recv, l_send, l_recv, p_send, p_recv, c_send, c_recv):
    heads, length, width = local_ref.shape
    owned = slot_ref.shape[0]
    me = lax.axis_index("seq")
    head_at = lax.axis_index("head")
    rep_at = lax.axis_index("rep")
    piece = layer_ref.shape[1]
    mesh_id = pl.DeviceIdType.MESH
    up, down, partner = {"seq": me + 1}, {"seq": me - 1}, {"rep": 1 - rep_at}
    has_up, has_down = me < n - 1, me > 0
    load = pltpu.make_async_copy(weight_hbm, weight, weight_sem)
    load.start()

    barrier = pltpu.get_barrier_semaphore()

    @pl.when(has_up)
    def _():
        pl.semaphore_signal(barrier, inc=1, device_id=up, device_id_type=mesh_id)

    @pl.when(has_down)
    def _():
        pl.semaphore_signal(barrier, inc=1, device_id=down, device_id_type=mesh_id)

    pl.semaphore_signal(barrier, inc=1, device_id=partner, device_id_type=mesh_id)
    for j in range(1, nh):
        pl.semaphore_signal(barrier, inc=1, device_id={"head": lax.rem(head_at + j, nh)}, device_id_type=mesh_id)

    inner = has_up & has_down

    @pl.when(inner)
    def _():
        pl.semaphore_wait(barrier, nh + 2)

    @pl.when(jnp.logical_not(inner))
    def _():
        pl.semaphore_wait(barrier, nh + 1)

    def remote(src, dst, send, recv, target):
        return pltpu.make_async_remote_copy(src_ref=src, dst_ref=dst, send_sem=send, recv_sem=recv,
                                            device_id=target, device_id_type=mesh_id)

    def state_copy(h):
        return remote(state_out.at[h], state_in.at[h], st_send.at[h], st_recv.at[h], up)

    def raw_up(h):
        return remote(own.at[h], raw_r.at[h], rr_send.at[h], rr_recv.at[h], up)

    def raw_down(h):
        return remote(own.at[h], raw_l.at[h], rl_send.at[h], rl_recv.at[h], down)

    def block_up(h, j):
        span = pl.ds(j * owned, owned)
        return remote(buf_r.at[h, span], buf_r.at[h, span], r_send.at[h, j], r_recv.at[h, j], up)

    def block_down(h, j):
        span = pl.ds(j * owned, owned)
        return remote(buf_l.at[h, span], buf_l.at[h, span], l_send.at[h, j], l_recv.at[h, j], down)

    def pair_copy(j):
        return remote(parts.at[2 * j + 1 - rep_at], pair_in.at[j], p_send.at[j], p_recv.at[j], partner)

    def cross_copy(j):
        return remote(sums.at[j], cross_in.at[j], c_send.at[j], c_recv.at[j],
                      {"head": lax.rem(head_at + j, nh)})

    open_flag = scal_ref[0]
    gain = gain_ref[...]

    @pl.when(me == 0)
    def _():
        state_in[...] = jnp.zeros_like(state_in)
        for h in range(heads):
            buf_r[h, :owned] = jnp.zeros((owned, width, width), BF16)

    @pl.when(me == n - 1)
    def _():
        for h in range(heads):
            buf_l[h, (n - 1) * owned:] = jnp.zeros((owned, width, width), BF16)

    def relay(h, carry):
        @pl.when(has_down)
        def _():
            state_copy(h).wait_recv()

        arriving = state_in[h]
        moved = jnp.dot(map_ref[h], arriving, preferred_element_type=F32)
        state_out[h] = (tail_ref[h] + open_flag * moved).astype(BF16)

        @pl.when(has_up)
        def _():
            state_copy(h).start()

        own[h, 0] = (end0_ref[h] + (1.0 - open_flag) * moved).astype(BF16)
        own[h, 1:] = rest_ref[h]

        @pl.when(me == 0)
        def _():
            raw_up(h).start()

        @pl.when(me == n - 1)
        def _():
            raw_down(h).start()

        out = local_ref[h] + jnp.dot(corr_ref[h], arriving, preferred_element_type=F32)
        cols = pl.ds(pl.multiple_of(h * width, width), width)
        scale = lax.rsqrt(jnp.mean(out * out, axis=-1, keepdims=True) + 1e-05)
        hidden[:, cols] = (out * scale * gain * jax.nn.sigmoid(gate_ref[:, cols].astype(F32))).astype(BF16)
        return carry

    lax.fori_loop(0, heads, relay, 0)

    def picked(ref, which, h, s):
        total = sel_ref[which, 0, s] * ref[h, 0].astype(F32)
        for e in range(1, ENDS_MAX):
            total = total + sel_ref[which, e, s] * ref[h, e].astype(F32)
        return total

    def stage(h, at_first, raw, buf, raw_copy, block_copy, which, dests, beyond, active):
        @pl.when(active & at_first)
        def _():
            raw_copy(h).wait_recv()

        for j in dests:
            mine = me == j
            further = beyond(j)

            @pl.when(active & at_first & (mine | further))
            def _():
                for s in range(j * owned, (j + 1) * owned):
                    buf[h, s] = picked(raw, which, h, s).astype(BF16)

            @pl.when(active & jnp.logical_not(at_first) & (mine | further))
            def _():
                block_copy(h, j).wait_recv()

            @pl.when(active & further)
            def _():
                for s in range(j * owned, (j + 1) * owned):
                    buf[h, s] = (buf[h, s].astype(F32) + picked(own, 0, h, s)).astype(BF16)
                block_copy(h, j).start()

    def exchange(h, carry):
        stage(h, me == 1, raw_r, buf_r, raw_up, block_up, 1, range(1, n), lambda j: j > me, me >= 1)
        stage(h, me == n - 2, raw_l, buf_l, raw_down, block_down, 2, range(n - 1), lambda j: j < me, me <= n - 2)
        for k in range(owned):
            s = me * owned + k
            slot_ref[k, h] = (picked(own, 0, h, s) + buf_r[h, s].astype(F32) + buf_l[h, s].astype(F32)).astype(BF16)
        return carry

    lead = heads // 4
    load.wait()
    full = jnp.dot(hidden[...], weight[...], preferred_element_type=F32)
    for d in range(2 * nh):
        parts[d] = full[:, d * piece:(d + 1) * piece].astype(BF16)
    for j in range(nh):
        pair_copy(j).start()
    lax.fori_loop(0, lead, exchange, 0)
    for j in range(nh):
        pair_copy(j).wait_recv()
    for j in range(1, nh):
        at = lax.rem(head_at + j, nh)
        sums[j] = (parts[2 * at + rep_at].astype(F32) + pair_in[at].astype(F32)).astype(BF16)
        cross_copy(j).start()
    lax.fori_loop(lead, heads, exchange, 0)
    result = parts[2 * head_at + rep_at].astype(F32) + pair_in[head_at].astype(F32)
    for j in range(1, nh):
        cross_copy(j).wait_recv()
        result = result + cross_in[j].astype(F32)
    layer_ref[...] = result.astype(BF16)

    for j in range(nh):
        pair_copy(j).wait_send()
    for j in range(1, nh):
        cross_copy(j).wait_send()

    def drain(h, carry):
        @pl.when(has_up)
        def _():
            state_copy(h).wait_send()

        @pl.when(me == 0)
        def _():
            raw_up(h).wait_send()

        @pl.when(me == n - 1)
        def _():
            raw_down(h).wait_send()

        for j in range(1, n):
            @pl.when((me >= 1) & (j > me))
            def _():
                block_up(h, j).wait_send()

        for j in range(n - 1):
            @pl.when((me <= n - 2) & (j < me))
            def _():
                block_down(h, j).wait_send()

        return carry

    lax.fori_loop(0, heads, drain, 0)


def finish(scal, sel, local, corr, maps, tail, end0, rest, gates, gain, weight, owned):
    n = lax.axis_size("seq")
    nh = lax.axis_size("head")
    heads, length, width = local.shape
    depth, model = weight.shape
    piece = model // (2 * nh)
    slots = n * owned
    vmem = pl.BlockSpec(memory_space=pltpu.VMEM)
    smem = pl.BlockSpec(memory_space=pltpu.SMEM)
    dma = pltpu.SemaphoreType.DMA
    cube = pltpu.VMEM((heads, width, width), BF16)
    quad = pltpu.VMEM((heads, ENDS_MAX, width, width), BF16)
    flow = pltpu.VMEM((heads, slots, width, width), BF16)
    return pl.pallas_call(
        functools.partial(finish_kernel, n, nh),
        out_shape=(jax.ShapeDtypeStruct((length, piece), BF16),
                   jax.ShapeDtypeStruct((owned, heads, width, width), BF16)),
        in_specs=[smem, smem] + [vmem] * 8 + [pl.BlockSpec(memory_space=pl.ANY)],
        out_specs=(vmem, vmem),
        scratch_shapes=[
            pltpu.VMEM((depth, model), BF16),
            pltpu.VMEM((length, depth), BF16),
            pltpu.VMEM((2 * nh, length, piece), BF16),
            pltpu.VMEM((nh, length, piece), BF16),
            pltpu.VMEM((nh, length, piece), BF16),
            pltpu.VMEM((nh, length, piece), BF16),
            cube, cube, quad, quad, quad, flow, flow,
            dma(()),
            dma((heads,)), dma((heads,)), dma((heads,)), dma((heads,)), dma((heads,)), dma((heads,)),
            dma((heads, n)), dma((heads, n)), dma((heads, n)), dma((heads, n)),
            dma((nh,)), dma((nh,)), dma((nh,)), dma((nh,)),
        ],
        compiler_params=pltpu.CompilerParams(collective_id=0, has_side_effects=True,
                                             vmem_limit_bytes=60 << 20),
        name="finish",
    )(scal, sel, local, corr, maps, tail, end0, rest, gates, gain.reshape(1, -1), weight)


def per_device(query_proj, key_proj, value_proj, forget_logits, decay_rate, beta_logits,
               gate_logits, norm_gain, out_weight, stream_starts, stream_slots):
    length = query_proj.shape[0]
    devices = lax.axis_size("seq")
    place = lax.axis_index("seq")
    anchor = place * length
    positions = anchor + jnp.arange(length, dtype=jnp.int32)
    count = lambda mask: jnp.sum(mask.astype(jnp.int32), axis=-1)
    segments = count(stream_starts[None, :] <= positions[:, None])
    before = jnp.where(place == 0, -1, count(stream_starts <= anchor - 1))
    later = stream_starts[1:]
    spots = place + jnp.array([0, -1, 1], jnp.int32)
    begins = spots[:, None] * length
    earlier = count(later[None] <= begins)
    ends = count((later[None] > begins) & (later[None] <= begins + length)) + (spots == devices - 1).astype(jnp.int32)
    total = stream_slots.shape[0]
    picks = jnp.arange(ENDS_MAX, dtype=jnp.int32)
    hit = ((jnp.arange(total, dtype=jnp.int32)[None, None, :] == (earlier[:, None] + picks[None, :])[:, :, None])
           & (picks[None, :] < ends[:, None])[:, :, None])
    places = jnp.sum(jnp.where(hit, stream_slots[None, None, :] + 1, 0), axis=-1) - 1
    sel = (places[:, :, None] == jnp.arange(total, dtype=jnp.int32)).astype(F32)
    scal = (ends[:1] == 0).astype(F32)
    local, corr, maps, tail, end0, rest = local_math(
        query_proj, key_proj, value_proj, forget_logits, decay_rate, beta_logits,
        segments, before, earlier[0] + 1, ends[0])
    return finish(scal, sel, local, corr, maps, tail, end0, rest, gate_logits, norm_gain, out_weight,
                  total // devices)


def solution(mesh):
    rows = P(("groups", "seq"), ("head", "rep"))
    in_specs = (rows, rows, rows, rows, P(("head", "rep")), rows, rows, P(),
                P(("head", "rep"), None), P("groups"), P("groups"))
    out_specs = (rows, P(("groups", "seq"), ("head", "rep"), None, None))
    return jax.shard_map(per_device, mesh=mesh, in_specs=in_specs, out_specs=out_specs, check_vma=False)
```

```python
import functools
import jax
import jax.numpy as jnp
from jax import lax
from jax.experimental import pallas as pl
from jax.experimental.pallas import tpu as pltpu
from jax.sharding import PartitionSpec as P

ENDS_MAX = 4
STEP_HEADS = 2
BASE = 16
F32 = jnp.float32
BF16 = jnp.bfloat16
NN = (((1,), (0,)), ((), ()))
NT = (((1,), (1,)), ((), ()))


def halves(x):
    high = x.astype(BF16)
    return high, (x - high.astype(F32)).astype(BF16)


def mm1(a, b, dims=NN):
    return lax.dot_general(a.astype(BF16), b.astype(BF16), dims, preferred_element_type=F32)


def mm3(a, b, dims=NN):
    ah, al = halves(a)
    bh, bl = halves(b)
    dot = functools.partial(lax.dot_general, dimension_numbers=dims, preferred_element_type=F32)
    return dot(ah, bh) + (dot(ah, bl) + dot(al, bh))


def unit(x):
    return x * lax.rsqrt(jnp.sum(x * x, axis=-1, keepdims=True) + 1e-06)


def block_inverses(mats):
    size = mats[0].shape[0]
    row = lax.broadcasted_iota(jnp.int32, (size, size), 0)
    col = lax.broadcasted_iota(jnp.int32, (size, size), 1)
    eye = (row == col).astype(F32)
    inside = (row // BASE) == (col // BASE)
    powers = [jnp.where(inside, m, 0.0) for m in mats]
    result = [eye - p for p in powers]
    width = 2
    while width < BASE:
        powers = [mm3(p, p) for p in powers]
        result = [r + mm3(r, p) for r, p in zip(result, powers)]
        width *= 2
    width = BASE
    while width < size:
        off = ((row // (2 * width)) == (col // (2 * width))) & ((row // width) > (col // width))
        mids = [mm3(jnp.where(off, m, 0.0), r) for m, r in zip(mats, result)]
        result = [r - mm3(r, t) for r, t in zip(result, mids)]
        width *= 2
    return result


def local_kernel(info_ref, q_ref, k_ref, v_ref, f_ref, rate_ref, beta_ref, seg_col_ref, seg_row_ref,
                 out_ref, corr_ref, map_ref, tail_ref, end0_ref, ends_ref):
    length = q_ref.shape[0]
    half = length // 2
    step = pl.program_id(0)
    width = q_ref.shape[1] // STEP_HEADS
    before = info_ref[0]
    base = info_ref[1]
    ends = info_ref[2]
    seg_col = seg_col_ref[...]
    seg_row = seg_row_ref[...]
    row = lax.broadcasted_iota(jnp.int32, (length, length), 0)
    col = lax.broadcasted_iota(jnp.int32, (length, length), 1)
    same = seg_col == seg_row
    lower = same & (row >= col)
    strict = same & (row > col)
    first = (seg_col == before).astype(F32)
    first_row = (seg_row == before).astype(F32)
    sums = jnp.concatenate([(row >= col).astype(BF16), (same & (col > row)).astype(BF16)], axis=0)
    hrow = lax.broadcasted_iota(jnp.int32, (width, width), 0)
    hcol = lax.broadcasted_iota(jnp.int32, (width, width), 1)
    eye = (hrow == hcol).astype(F32)
    beta_all = jax.nn.sigmoid(beta_ref[...].astype(F32))
    lane = lax.broadcasted_iota(jnp.int32, beta_all.shape, 1)
    any_first = jnp.max(first_row)
    select = [
        ((seg_row == base + e) & (e < ends)).astype(F32) for e in range(ENDS_MAX)
    ] + [(seg_row == base + ends).astype(F32)]
    mats = []
    kept = []
    for i in range(STEP_HEADS):
        cols = slice(i * width, (i + 1) * width)
        q = unit(q_ref[:, cols].astype(F32))
        k = unit(k_ref[:, cols].astype(F32))
        x = f_ref[:, cols].astype(F32)
        soft = jnp.maximum(x, 0.0) + jnp.log1p(jnp.exp(-jnp.abs(x)))
        decay = -(rate_ref[:, cols] * soft)
        dh, dl = halves(decay)
        both = jnp.concatenate([dh, dl], axis=1)
        summed = lax.dot_general(sums, both, NN, preferred_element_type=F32)
        summed = summed[:, :width] + summed[:, width:]
        cum = summed[:length]
        suffix = jnp.exp(summed[length:])
        decayed = jnp.exp(cum)
        beta = jnp.sum(jnp.where(lane == step * STEP_HEADS + i, beta_all, 0.0), axis=1, keepdims=True)
        mid = cum[half - 1:half]
        parts = []
        scale = []
        for b in range(2):
            piece = cum[b * half:(b + 1) * half]
            center = 0.5 * (piece[:1] + piece[-1:])
            up = jnp.exp(piece - center)
            down = jnp.exp(center - piece)
            kb = k[b * half:(b + 1) * half]
            qb = q[b * half:(b + 1) * half]
            parts.append((jnp.concatenate([kb * up, qb * up], axis=0), kb * down))
            scale.append(center)
        blocks = [mm3(parts[b][0], parts[b][1], NT) for b in range(2)]
        cross = mm3(parts[1][0] * jnp.exp(scale[1] - mid), parts[0][1] * jnp.exp(mid - scale[0]), NT)
        coupling = [
            jnp.where(strict[b * half:(b + 1) * half, b * half:(b + 1) * half], blocks[b][:half], 0.0)
            * beta[b * half:(b + 1) * half]
            for b in range(2)
        ]
        coupling_cross = jnp.where(same[half:, :half], cross[:half], 0.0) * beta[half:]
        reading0 = jnp.where(lower[:half, :half], blocks[0][half:], 0.0)
        reading1 = jnp.where(lower[half:, half:], blocks[1][half:], 0.0)
        reading_cross = jnp.where(same[half:, :half], cross[half:], 0.0)
        right = jnp.concatenate([v_ref[:, cols].astype(F32) * beta, k * decayed * (beta * first)], axis=1)
        keep_row = jnp.exp(jnp.sum(first * decay, axis=0, keepdims=True))
        mats += coupling
        kept.append((coupling_cross, reading0, reading1, reading_cross, right,
                     q * decayed * first, (k * suffix).T, eye * (keep_row * any_first)))
    inverses = block_inverses(mats)
    for i in range(STEP_HEADS):
        cols = slice(i * width, (i + 1) * width)
        coupling_cross, reading0, reading1, reading_cross, right, query, key_end, diag = kept[i]
        u0 = mm3(inverses[2 * i], right[:half])
        u1 = mm3(inverses[2 * i + 1], right[half:] - mm3(coupling_cross, u0))
        u = jnp.concatenate([u0, u1], axis=0)
        r0 = mm3(reading0, u0)
        r1 = mm3(jnp.concatenate([reading_cross, reading1], axis=1), u)
        read = jnp.concatenate([r0, r1], axis=0)
        out_ref[i] = read[:, :width]
        corr_ref[i] = (query - read[:, width:]).astype(corr_ref.dtype)
        lhs = jnp.concatenate([key_end * m for m in select], axis=0)
        states = mm1(lhs, u[:, :width])
        map_ref[i] = (diag - mm1(key_end * first_row, u[:, width:])).astype(map_ref.dtype)
        tail_ref[i] = states[ENDS_MAX * width:]
        end0_ref[i] = states[:width]
        for e in range(1, ENDS_MAX):
            ends_ref[i, e - 1] = states[e * width:(e + 1) * width].astype(BF16)


def local_math(q, k, v, f, rate, beta, seg, before, base, ends):
    length, total = q.shape
    heads = beta.shape[1]
    width = total // heads
    steps = heads // STEP_HEADS
    wide = pl.BlockSpec((length, STEP_HEADS * width), lambda n, s: (0, n))
    whole = lambda shape: pl.BlockSpec(shape, lambda n, s: (0, 0))
    cube = pl.BlockSpec((STEP_HEADS, width, width), lambda n, s: (n, 0, 0))
    info = jnp.stack([before, base, ends]).astype(jnp.int32)
    return pl.pallas_call(
        local_kernel,
        out_shape=(
            jax.ShapeDtypeStruct((heads, length, width), F32),
            jax.ShapeDtypeStruct((heads, length, width), BF16),
            jax.ShapeDtypeStruct((heads, width, width), BF16),
            jax.ShapeDtypeStruct((heads, width, width), F32),
            jax.ShapeDtypeStruct((heads, width, width), F32),
            jax.ShapeDtypeStruct((heads, ENDS_MAX - 1, width, width), BF16),
        ),
        grid_spec=pltpu.PrefetchScalarGridSpec(
            num_scalar_prefetch=1,
            grid=(steps,),
            in_specs=[wide, wide, wide, wide, pl.BlockSpec((1, STEP_HEADS * width), lambda n, s: (0, n)),
                      whole((length, heads)), whole((length, 1)), whole((1, length))],
            out_specs=(
                pl.BlockSpec((STEP_HEADS, length, width), lambda n, s: (n, 0, 0)),
                pl.BlockSpec((STEP_HEADS, length, width), lambda n, s: (n, 0, 0)),
                cube, cube, cube,
                pl.BlockSpec((STEP_HEADS, ENDS_MAX - 1, width, width), lambda n, s: (n, 0, 0, 0)),
            ),
        ),
        compiler_params=pltpu.CompilerParams(vmem_limit_bytes=48 << 20),
        name="local_math",
    )(info, q, k, v, f, rate.reshape(1, -1), beta, seg.reshape(-1, 1), seg.reshape(1, -1))


LAG = 2


def finish_kernel(n, nh, scal_ref, sel_ref, gain_ref, local_hbm, corr_hbm, map_hbm, tail_hbm, end0_hbm, rest_hbm,
                  gate_hbm, weight_hbm, layer_ref, slot_ref,
                  local_ref, corr_ref, map_ref, tail_ref, end0_ref, gate_ref, weight, hidden, parts, sums, pair_in, cross_in, state_out, state_in, own,
                  raw_r, raw_l, buf_r, buf_l,
                  load_sem, st_send, st_recv, rr_send, rr_recv, rl_send, rl_recv,
                  qr_send, qr_recv, ql_send, ql_recv,
                  r_send, r_recv, l_send, l_recv, p_send, p_recv, c_send, c_recv):
    heads, length, width = local_ref.shape
    owned = slot_ref.shape[0]
    me = lax.axis_index("seq")
    head_at = lax.axis_index("head")
    rep_at = lax.axis_index("rep")
    piece = layer_ref.shape[1]
    mesh_id = pl.DeviceIdType.MESH
    up, down, partner = {"seq": me + 1}, {"seq": me - 1}, {"rep": 1 - rep_at}
    has_up, has_down = me < n - 1, me > 0
    pairs = ((rest_hbm, own.at[:, pl.ds(1, ENDS_MAX - 1)]), (map_hbm, map_ref), (tail_hbm, tail_ref),
             (end0_hbm, end0_ref), (local_hbm, local_ref), (corr_hbm, corr_ref), (gate_hbm, gate_ref),
             (weight_hbm, weight))
    loads = [pltpu.make_async_copy(src, dst, load_sem.at[i]) for i, (src, dst) in enumerate(pairs)]
    for load in loads:
        load.start()

    barrier = pltpu.get_barrier_semaphore()

    @pl.when(has_up)
    def _():
        pl.semaphore_signal(barrier, inc=1, device_id=up, device_id_type=mesh_id)

    @pl.when(has_down)
    def _():
        pl.semaphore_signal(barrier, inc=1, device_id=down, device_id_type=mesh_id)

    pl.semaphore_signal(barrier, inc=1, device_id=partner, device_id_type=mesh_id)
    for j in range(1, nh):
        pl.semaphore_signal(barrier, inc=1, device_id={"head": lax.rem(head_at + j, nh)}, device_id_type=mesh_id)

    inner = has_up & has_down

    @pl.when(inner)
    def _():
        pl.semaphore_wait(barrier, nh + 2)

    @pl.when(jnp.logical_not(inner))
    def _():
        pl.semaphore_wait(barrier, nh + 1)

    def remote(src, dst, send, recv, target):
        return pltpu.make_async_remote_copy(src_ref=src, dst_ref=dst, send_sem=send, recv_sem=recv,
                                            device_id=target, device_id_type=mesh_id)

    def state_copy(h):
        return remote(state_out.at[h], state_in.at[h], st_send.at[h], st_recv.at[h], up)

    def raw_up(h):
        return remote(own.at[h, pl.ds(0, 1)], raw_r.at[h, pl.ds(0, 1)], rr_send.at[h], rr_recv.at[h], up)

    def raw_down(h):
        return remote(own.at[h, pl.ds(0, 1)], raw_l.at[h, pl.ds(0, 1)], rl_send.at[h], rl_recv.at[h], down)

    others = pl.ds(1, ENDS_MAX - 1)

    def others_up(h):
        return remote(own.at[h, others], raw_r.at[h, others], qr_send.at[h], qr_recv.at[h], up)

    def others_down(h):
        return remote(own.at[h, others], raw_l.at[h, others], ql_send.at[h], ql_recv.at[h], down)

    def block_up(h, j):
        span = pl.ds(j * owned, owned)
        return remote(buf_r.at[h, span], buf_r.at[h, span], r_send.at[h, j], r_recv.at[h, j], up)

    def block_down(h, j):
        span = pl.ds(j * owned, owned)
        return remote(buf_l.at[h, span], buf_l.at[h, span], l_send.at[h, j], l_recv.at[h, j], down)

    def pair_copy(j):
        return remote(parts.at[2 * j + 1 - rep_at], pair_in.at[j], p_send.at[j], p_recv.at[j], partner)

    def cross_copy(j):
        return remote(sums.at[j], cross_in.at[j], c_send.at[j], c_recv.at[j],
                      {"head": lax.rem(head_at + j, nh)})

    open_flag = scal_ref[0]
    gain = gain_ref[...]

    @pl.when(me == 0)
    def _():
        state_in[...] = jnp.zeros_like(state_in)
        for h in range(heads):
            buf_r[h, :owned] = jnp.zeros((owned, width, width), BF16)

    @pl.when(me == n - 1)
    def _():
        for h in range(heads):
            buf_l[h, (n - 1) * owned:] = jnp.zeros((owned, width, width), BF16)

    loads[0].wait()

    def early(h, carry):
        @pl.when(me == 0)
        def _():
            others_up(h).start()

        @pl.when(me == n - 1)
        def _():
            others_down(h).start()

        return carry

    lax.fori_loop(0, heads, early, 0)
    for load in loads[1:-1]:
        load.wait()

    def relay(h, carry):
        @pl.when(has_down)
        def _():
            state_copy(h).wait_recv()

        arriving = state_in[h]
        moved = jnp.dot(map_ref[h], arriving, preferred_element_type=F32)
        state_out[h] = (tail_ref[h] + open_flag * moved).astype(BF16)

        @pl.when(has_up)
        def _():
            state_copy(h).start()

        own[h, 0] = (end0_ref[h] + (1.0 - open_flag) * moved).astype(BF16)

        @pl.when(me == 0)
        def _():
            raw_up(h).start()

        @pl.when(me == n - 1)
        def _():
            raw_down(h).start()

        out = local_ref[h] + jnp.dot(corr_ref[h], arriving, preferred_element_type=F32)
        cols = pl.ds(pl.multiple_of(h * width, width), width)
        scale = lax.rsqrt(jnp.mean(out * out, axis=-1, keepdims=True) + 1e-05)
        hidden[:, cols] = (out * scale * gain * jax.nn.sigmoid(gate_ref[:, cols].astype(F32))).astype(BF16)
        return carry

    lax.fori_loop(0, heads, relay, 0)

    def picked(ref, which, h, s):
        total = sel_ref[which, 0, s] * ref[h, 0].astype(F32)
        for e in range(1, ENDS_MAX):
            total = total + sel_ref[which, e, s] * ref[h, e].astype(F32)
        return total

    def stage(h, at_first, raw, buf, raw_copy, others_copy, block_copy, which, dests, beyond, active):
        @pl.when(active & at_first)
        def _():
            others_copy(h).wait_recv()
            raw_copy(h).wait_recv()

        for j in dests:
            mine = me == j
            further = beyond(j)

            @pl.when(active & at_first & (mine | further))
            def _():
                for s in range(j * owned, (j + 1) * owned):
                    buf[h, s] = picked(raw, which, h, s).astype(BF16)

            @pl.when(active & jnp.logical_not(at_first) & (mine | further))
            def _():
                block_copy(h, j).wait_recv()

            @pl.when(active & further)
            def _():
                for s in range(j * owned, (j + 1) * owned):
                    buf[h, s] = (buf[h, s].astype(F32) + picked(own, 0, h, s)).astype(BF16)
                block_copy(h, j).start()

    def exchange(t, carry):
        hr = t - LAG * (me - 1)
        hl = t - LAG * (n - 2 - me)
        hf = t - LAG * (n - 2)

        @pl.when((me >= 1) & (hr >= 0) & (hr < heads))
        def _():
            stage(hr, me == 1, raw_r, buf_r, raw_up, others_up, block_up, 1, range(1, n), lambda j: j > me, me >= 1)

        @pl.when((me <= n - 2) & (hl >= 0) & (hl < heads))
        def _():
            stage(hl, me == n - 2, raw_l, buf_l, raw_down, others_down, block_down, 2, range(n - 1),
                  lambda j: j < me, me <= n - 2)

        @pl.when((hf >= 0) & (hf < heads))
        def _():
            for k in range(owned):
                s = me * owned + k
                slot_ref[k, hf] = (picked(own, 0, hf, s) + buf_r[hf, s].astype(F32)
                                   + buf_l[hf, s].astype(F32)).astype(BF16)

        return carry

    lead = max(heads // 4, 1)
    loads[-1].wait()
    full = jnp.dot(hidden[...], weight[...], preferred_element_type=F32)
    for d in range(2 * nh):
        parts[d] = full[:, d * piece:(d + 1) * piece].astype(BF16)
    for j in range(nh):
        pair_copy(j).start()
    lax.fori_loop(0, lead, exchange, 0)
    for j in range(nh):
        pair_copy(j).wait_recv()
    for j in range(1, nh):
        at = lax.rem(head_at + j, nh)
        sums[j] = (parts[2 * at + rep_at].astype(F32) + pair_in[at].astype(F32)).astype(BF16)
        cross_copy(j).start()
    lax.fori_loop(lead, heads + LAG * (n - 2), exchange, 0)
    result = parts[2 * head_at + rep_at].astype(F32) + pair_in[head_at].astype(F32)
    for j in range(1, nh):
        cross_copy(j).wait_recv()
        result = result + cross_in[j].astype(F32)
    layer_ref[...] = result.astype(BF16)

    for j in range(nh):
        pair_copy(j).wait_send()
    for j in range(1, nh):
        cross_copy(j).wait_send()

    def drain(h, carry):
        @pl.when(has_up)
        def _():
            state_copy(h).wait_send()

        @pl.when(me == 0)
        def _():
            raw_up(h).wait_send()
            others_up(h).wait_send()

        @pl.when(me == n - 1)
        def _():
            raw_down(h).wait_send()
            others_down(h).wait_send()

        for j in range(1, n):
            @pl.when((me >= 1) & (j > me))
            def _():
                block_up(h, j).wait_send()

        for j in range(n - 1):
            @pl.when((me <= n - 2) & (j < me))
            def _():
                block_down(h, j).wait_send()

        return carry

    lax.fori_loop(0, heads, drain, 0)


def finish(scal, sel, local, corr, maps, tail, end0, rest, gates, gain, weight, owned):
    n = lax.axis_size("seq")
    nh = lax.axis_size("head")
    heads, length, width = local.shape
    depth, model = weight.shape
    piece = model // (2 * nh)
    slots = n * owned
    vmem = pl.BlockSpec(memory_space=pltpu.VMEM)
    smem = pl.BlockSpec(memory_space=pltpu.SMEM)
    dma = pltpu.SemaphoreType.DMA
    cube = pltpu.VMEM((heads, width, width), BF16)
    quad = pltpu.VMEM((heads, ENDS_MAX, width, width), BF16)
    flow = pltpu.VMEM((heads, slots, width, width), BF16)
    return pl.pallas_call(
        functools.partial(finish_kernel, n, nh),
        out_shape=(jax.ShapeDtypeStruct((length, piece), BF16),
                   jax.ShapeDtypeStruct((owned, heads, width, width), BF16)),
        in_specs=[smem, smem, vmem] + [pl.BlockSpec(memory_space=pl.ANY)] * 8,
        out_specs=(vmem, vmem),
        scratch_shapes=[
            pltpu.VMEM(local.shape, F32),
            pltpu.VMEM(corr.shape, BF16),
            pltpu.VMEM(maps.shape, BF16),
            pltpu.VMEM(tail.shape, F32),
            pltpu.VMEM(end0.shape, F32),
            pltpu.VMEM(gates.shape, BF16),
            pltpu.VMEM((depth, model), BF16),
            pltpu.VMEM((length, depth), BF16),
            pltpu.VMEM((2 * nh, length, piece), BF16),
            pltpu.VMEM((nh, length, piece), BF16),
            pltpu.VMEM((nh, length, piece), BF16),
            pltpu.VMEM((nh, length, piece), BF16),
            cube, cube, quad, quad, quad, flow, flow,
            dma((8,)),
            dma((heads,)), dma((heads,)), dma((heads,)), dma((heads,)),
            dma((heads,)), dma((heads,)), dma((heads,)), dma((heads,)), dma((heads,)), dma((heads,)),
            dma((heads, n)), dma((heads, n)), dma((heads, n)), dma((heads, n)),
            dma((nh,)), dma((nh,)), dma((nh,)), dma((nh,)),
        ],
        compiler_params=pltpu.CompilerParams(collective_id=0, has_side_effects=True,
                                             vmem_limit_bytes=60 << 20),
        name="finish",
    )(scal, sel, gain.reshape(1, -1), local, corr, maps, tail, end0, rest, gates, weight)


def per_device(query_proj, key_proj, value_proj, forget_logits, decay_rate, beta_logits,
               gate_logits, norm_gain, out_weight, stream_starts, stream_slots):
    length = query_proj.shape[0]
    devices = lax.axis_size("seq")
    place = lax.axis_index("seq")
    anchor = place * length
    positions = anchor + jnp.arange(length, dtype=jnp.int32)
    count = lambda mask: jnp.sum(mask.astype(jnp.int32), axis=-1)
    segments = count(stream_starts[None, :] <= positions[:, None])
    before = jnp.where(place == 0, -1, count(stream_starts <= anchor - 1))
    later = stream_starts[1:]
    spots = place + jnp.array([0, -1, 1], jnp.int32)
    begins = spots[:, None] * length
    earlier = count(later[None] <= begins)
    ends = count((later[None] > begins) & (later[None] <= begins + length)) + (spots == devices - 1).astype(jnp.int32)
    total = stream_slots.shape[0]
    picks = jnp.arange(ENDS_MAX, dtype=jnp.int32)
    hit = ((jnp.arange(total, dtype=jnp.int32)[None, None, :] == (earlier[:, None] + picks[None, :])[:, :, None])
           & (picks[None, :] < ends[:, None])[:, :, None])
    places = jnp.sum(jnp.where(hit, stream_slots[None, None, :] + 1, 0), axis=-1) - 1
    sel = (places[:, :, None] == jnp.arange(total, dtype=jnp.int32)).astype(F32)
    scal = (ends[:1] == 0).astype(F32)
    local, corr, maps, tail, end0, rest = local_math(
        query_proj, key_proj, value_proj, forget_logits, decay_rate, beta_logits,
        segments, before, earlier[0] + 1, ends[0])
    return finish(scal, sel, local, corr, maps, tail, end0, rest, gate_logits, norm_gain, out_weight,
                  total // devices)


def solution(mesh):
    rows = P(("groups", "seq"), ("head", "rep"))
    in_specs = (rows, rows, rows, rows, P(("head", "rep")), rows, rows, P(),
                P(("head", "rep"), None), P("groups"), P("groups"))
    out_specs = (rows, P(("groups", "seq"), ("head", "rep"), None, None))
    return jax.shard_map(per_device, mesh=mesh, in_specs=in_specs, out_specs=out_specs, check_vma=False)
```
